32 devices in a mesh: group: 2 (over y), sample: 8 (over z, x), mode: 2 (over core).
Axes of the slice: x: 2, y: 2, z: 4, core: 2. Of those that a mesh axis runs over, the one named last changes fastest.
Arguments:
- displace: bfloat16 [8192, 3072], P(('group', 'sample')), parts along dimension 0, may hold values from -6 to 6
- forces: bfloat16 [8192, 3072], P(('group', 'sample'), 'mode'), parts along dimension 0, may hold values from -6 to 6
- trial: bfloat16 [6144, 512], P(('group', 'sample'), 'mode'), parts along dimension 0, may hold values from -0.109375 to 0.109375
Outputs:
- hess_block: float32 [6144, 512], P(('group', 'sample'), 'mode'), parts along dimension 0
The draws below stay inside these ranges and needn't reach their ends.
There are 2 independent parts, one for each index of `group`. The reference program is written for one: setup_inputs(seed, part) draws one part's arguments, and reference() takes and returns one part's arrays. A program takes and returns all parts, laid end to end along the dimension named above; each array names one. Nothing has to cross between parts.
All inputs are finite; a program needn't handle non-finite values.
Results may differ from the reference program's by a relative error of at most 0.0028.
Values may be sent and summed in bfloat16 or wider, within the bound.
No kernel may reach another device: no remote copies, remote signals or barrier semaphores. Data moves between devices by JAX's collectives and lax.ppermute only.
A program may use at most 64 MiB of HBM per device.

```python
import math
import jax
import jax.numpy as jnp
from jax import lax

M = 3072
K = 512
SAMPLES = 4096


def raised(entries, own_key, source, target, blocks, factor):
    def block_of(dim):
        return (jnp.arange(entries.shape[dim]) // (entries.shape[dim] // blocks)).reshape((-1,) + (1,) * (entries.ndim - 1 - dim))

    one_side = jax.random.permutation(own_key, blocks)[block_of(target)]
    far = (block_of(target) + blocks // 2) % blocks
    return jnp.where((block_of(source) == one_side) | (block_of(source) == far), factor * entries, entries)


def levels(key, shape, pieces, least, largest):
    level = 1.0
    for axis_at, shards_of in pieces:
        draws = jax.random.uniform(jax.random.fold_in(jax.random.fold_in(key, 6), axis_at), (shards_of,), jnp.float32, least / len(pieces), largest / len(pieces))
        level = level * jnp.repeat(jnp.exp(draws), shape[axis_at] // shards_of).reshape((-1,) + (1,) * (len(shape) - 1 - axis_at))
    return level


def gaussian(rng, dims, spread, reach, cuts=(), held_as=jnp.bfloat16):
    loudness = levels(rng, dims, cuts, -0.22, 0.18) if cuts else 1.0
    array = jax.random.normal(rng, dims, jnp.float32) * spread * loudness
    return jnp.minimum(jnp.maximum(array, -reach), reach).astype(held_as)


def gaussian_with(own_key, shape, spread, bound, pieces, heavy, dtype=jnp.bfloat16):
    values = spread * jax.random.normal(own_key, shape, jnp.float32)
    if pieces:
        values = values * levels(own_key, shape, pieces, -0.22, 0.18)
    return jnp.clip(raised(values, jax.random.fold_in(own_key, 3), *heavy), -bound, bound).astype(dtype)


def setup_inputs(seed: int = 0, part: int = 0) -> dict:
    key_list = jax.random.split(jax.random.key(seed), 4)
    part_splits = jax.random.split(jax.random.fold_in(key_list[3], part), 4)
    displace = gaussian_with(part_splits[0], (SAMPLES, M), 1.0, 6.0, ((0, 8),), (0, 1, 8, 2.0))
    forces = gaussian(part_splits[1], (SAMPLES, M), 1.0, 6.0, ((0, 8), (1, 2)))
    trial = gaussian(part_splits[2], (M, K), M ** -0.5, 0.109375, ((0, 8), (1, 2)))
    return dict(displace=displace, forces=forces, trial=trial)


def reference(displace, forces, trial):
    proj_x = jnp.dot(displace, trial, preferred_element_type=jnp.float32)
    proj_f = jnp.dot(forces, trial, preferred_element_type=jnp.float32)
    weights = lax.optimization_barrier(jnp.sum(displace.astype(jnp.float32) * forces.astype(jnp.float32), axis=1)) / math.sqrt(M)
    scaled_x = (weights[:, None] * proj_x).astype(jnp.bfloat16)
    scaled_f = (weights[:, None] * proj_f).astype(jnp.bfloat16)
    left = jnp.dot(displace.T, scaled_f, preferred_element_type=jnp.float32)
    right = jnp.dot(forces.T, scaled_x, preferred_element_type=jnp.float32)
    return (left + right) / (2.0 * math.sqrt(SAMPLES))
```

```python
import math

import jax
import jax.numpy as jnp
from jax import lax
from jax.sharding import PartitionSpec as P


PIECES = 8


def swap(value, axis, mask):
    size = lax.axis_size(axis)
    return lax.ppermute(value, axis, [(i, i ^ mask) for i in range(size)])


def contract_rows(columns, scaled):
    return lax.dot_general(
        columns, scaled, (((0,), (0,)), ((), ())), preferred_element_type=jnp.float32
    )


def shards(displace, forces, trial):
    ranks = lax.axis_size("sample")
    count = min(PIECES, ranks)
    inner = ranks // count
    teams = [[t * inner + i for i in range(inner)] for t in range(count)]
    me = lax.axis_index("sample") // inner
    if inner > 1:
        trial = lax.all_gather(trial, "sample", axis_index_groups=teams, axis=0, tiled=True)
    side = lax.axis_index("mode")
    samples, modes = displace.shape
    rows = trial.shape[0]
    other = swap(forces, "mode", 1)
    first = jnp.where(side == 0, forces, other)
    second = jnp.where(side == 0, other, forces)
    full = jnp.concatenate([first, second], axis=1)
    both = jnp.concatenate([displace, full], axis=0)
    weights = jnp.sum(
        displace.astype(jnp.float32) * full.astype(jnp.float32), axis=1
    ) / math.sqrt(modes)

    def columns_of(r):
        return lax.dynamic_slice_in_dim(both, (me ^ r) * rows, rows, 1)

    masks = [1 << b for b in range(count.bit_length() - 1)]
    blocks = {0: trial}
    for mask in reversed(masks):
        for r in sorted(blocks):
            blocks[r | mask] = swap(blocks[r], "sample", mask * inner)
    proj = None
    for r in sorted(blocks, key=lambda r: (r & 1, r)):
        term = jnp.dot(columns_of(r), blocks[r], preferred_element_type=jnp.float32)
        proj = term if proj is None else proj + term
    scaled_x = (weights[:, None] * proj[:samples]).astype(jnp.bfloat16)
    scaled_f = (weights[:, None] * proj[samples:]).astype(jnp.bfloat16)
    crossed = jnp.concatenate([scaled_f, scaled_x], axis=0)
    sums = {}
    for r in reversed(range(count)):
        sums[r] = contract_rows(columns_of(r), crossed)
    for mask in masks:
        for r in sorted(sums, reverse=True):
            if r & mask:
                sent = swap(sums.pop(r).astype(jnp.bfloat16), "sample", mask * inner)
                sums[r ^ mask] = sums[r ^ mask] + sent.astype(jnp.float32)
    result = sums[0]
    if inner > 1:
        result = lax.psum_scatter(
            result, "sample", scatter_dimension=0, axis_index_groups=teams, tiled=True
        )
    return result / (2.0 * math.sqrt(samples * ranks))


def solution(mesh):
    return jax.shard_map(
        shards,
        mesh=mesh,
        in_specs=(
            P(("group", "sample"), None),
            P(("group", "sample"), "mode"),
            P(("group", "sample"), "mode"),
        ),
        out_specs=P(("group", "sample"), "mode"),
        check_vma=False,
    )
```
